32 devices in a mesh: level: 8 (over z, y), bal: 4 (over x, core).
Axes of the slice: x: 2, y: 2, z: 4, core: 2. Of those that a mesh axis runs over, the one named last changes fastest.
Arguments:
- patches: float32 [640, 5, 4096], P(('level', 'bal')), may hold values from -6 to 6
- patch_ids: int32 [640], P(('level', 'bal')), may hold values from 0 to 639, each once
- live: int32 [32], P(('level', 'bal')), may hold values from 4 to 12, as said below
- counts: int32 [2, 32], P(None, ('level', 'bal')), may hold values from 0 to 4, as said below
- parent_of: int32 [640], replicated, may hold values from 0 to 15
Outputs:
- new_patches: float32 [640, 5, 4096], P(('level', 'bal'))
- new_ids: int32 [640], P(('level', 'bal'))
- coarse: float32 [16, 5, 512], P('level')
The draws below stay inside these ranges and needn't reach their ends.
Inputs may be any that keep to these rules, and one draw needn't show every extreme that they name: In every level group one device holds exactly 12 live patches. counts[r, d] never exceeds the live patches of device d at the start of round r; in every round and level group some device sends exactly 4.
All inputs are finite; a program needn't handle non-finite values.
Results may differ from the reference program's by a relative error of at most 0.0003.
Values sent between devices are 32-bit elements; how exact they have to be, the bound alone decides.
A program may use at most 64 MiB of HBM per device.

```python
import jax
import jax.numpy as jnp
import numpy as np

EDGE = 16
VARS = 5
SEND_MOST = 4
LOAD_MOST = 12
ROUNDS = 2
GROUP = 4
LEVELS = 8
CAP = 20
SLOTS = 640
CELLS = 4096
COARSE = 512
PARENTS = 16


def plan_layout(key):
    first_key = jax.random.fold_in(key, 11)
    second_key = jax.random.fold_in(key, 12)
    third_key = jax.random.fold_in(key, 13)
    members = jnp.arange(GROUP, dtype=jnp.int32)
    loads = jax.random.randint(first_key, (LEVELS, GROUP), SEND_MOST, LOAD_MOST + 1)
    heavy = jax.random.randint(second_key, (LEVELS,), 0, GROUP)
    light = (heavy + 1 + jax.random.randint(third_key, (LEVELS,), 0, GROUP - 1)) % GROUP
    loads = jnp.where(members[None, :] == heavy[:, None], LOAD_MOST, loads)
    loads = jnp.where(members[None, :] == light[:, None], SEND_MOST, loads)
    held_count = loads
    sends = []
    for turn_index in range(ROUNDS):
        turn_key = jax.random.fold_in(key, 100 + turn_index)
        limit = jnp.minimum(SEND_MOST, held_count)
        drawn = jax.random.randint(turn_key, (LEVELS, GROUP), SEND_MOST // 2, SEND_MOST + 1)
        sent_count = jnp.minimum(drawn, limit)
        breaker = jax.random.permutation(jax.random.fold_in(turn_key, 7), GROUP).astype(jnp.int32)
        score = held_count * GROUP + breaker[None, :]
        busiest = jnp.argmax(score, axis=1).astype(jnp.int32)
        sent_count = jnp.where(members[None, :] == busiest[:, None], limit, sent_count)
        partner = members ^ 1 << turn_index
        held_count = held_count - sent_count + sent_count[:, partner]
        sends.append(sent_count)
    return (loads.reshape(LEVELS * GROUP), jnp.stack(sends).reshape(ROUNDS, LEVELS * GROUP))


def draw_live(key, part):
    return plan_layout(key)[0].astype(jnp.int32)


def draw_counts(key, part):
    return plan_layout(key)[1].astype(jnp.int32)


def place_ends(values, own_key, smallest, largest):
    longest = values.shape.index(max(values.shape))
    spots = []
    for shift in (0, 1):
        where = [jax.random.randint(jax.random.fold_in(own_key, axis), (), 0, length) for axis, length in enumerate(values.shape)]
        where[longest] = (where[longest] + shift) % values.shape[longest]
        spots.append(tuple(where))
    return values.at[spots[0]].set(smallest).at[spots[1]].set(largest)


def level_of(stream_key, shape, pieces, low, high):
    def one(position, shards_of):
        draws = jax.random.uniform(jax.random.fold_in(jax.random.fold_in(stream_key, 6), position), (shards_of,), jnp.float32, low / len(pieces), high / len(pieces))
        return jnp.repeat(jnp.exp(draws), shape[position] // shards_of).reshape((-1,) + (1,) * (len(shape) - position - 1))

    loudness = one(*pieces[0])
    for cut in pieces[1:]:
        loudness = loudness * one(*cut)
    return loudness


def bell_draw(rng, dims, width, most, split=(), held_as=jnp.bfloat16):
    values = width * jax.random.normal(rng, dims, jnp.float32)
    if split:
        values = values * level_of(rng, dims, split, -0.22, 0.18)
    return jnp.clip(values, -most, most).astype(held_as)


def setup_inputs(seed: int = 0) -> dict:
    splits = jax.random.split(jax.random.key(seed), 6)
    patches = bell_draw(splits[0], (SLOTS, VARS, CELLS), 1.0, 6.0, ((0, 32),), jnp.float32)
    patch_ids = jax.random.permutation(splits[1], SLOTS).astype(jnp.int32)
    live = draw_live(jax.random.fold_in(splits[5], 71), 0)
    counts = draw_counts(jax.random.fold_in(splits[5], 71), 0)
    parent_of = place_ends(jax.random.randint(splits[4], (SLOTS,), 0, PARENTS), jax.random.fold_in(splits[4], 1), 0, PARENTS - 1).astype(jnp.int32)
    return {"patches": patches, "patch_ids": patch_ids, "live": live, "counts": counts, "parent_of": parent_of}


def restrict(fine_rows):
    leading = fine_rows.shape[:-1]
    half_edge = EDGE // 2
    blocks = fine_rows.reshape(leading + (half_edge, 2, half_edge, 2, half_edge, 2))
    return jnp.mean(blocks, axis=(-5, -3, -1)).reshape(leading + (half_edge * half_edge * half_edge,))


def take_top(fine_rows, fine_ids, held_count, sent_count):
    capacity = fine_rows.shape[0]
    lane_index = jnp.arange(SEND_MOST, dtype=jnp.int32)
    pick_index = jnp.clip(held_count - sent_count + lane_index, 0, capacity - 1)
    is_valid = lane_index < sent_count
    return (jnp.where(is_valid[:, None, None], fine_rows[pick_index], 0.0),
            jnp.where(is_valid, fine_ids[pick_index], -1))


def place_rows(fine_rows, fine_ids, kept_count, in_rows, in_ids):
    capacity = fine_rows.shape[0]
    slot_index = jnp.arange(capacity, dtype=jnp.int32)
    offset = slot_index - kept_count
    is_hit = (offset >= 0) & (offset < SEND_MOST)
    place_index = jnp.clip(offset, 0, SEND_MOST - 1)
    is_kept = slot_index < kept_count
    new_rows = jnp.where(is_kept[:, None, None], fine_rows,
                         jnp.where(is_hit[:, None, None], in_rows[place_index], 0.0))
    new_ids = jnp.where(is_kept, fine_ids, jnp.where(is_hit, in_ids[place_index], -1))
    return new_rows, new_ids


def reference(patches, patch_ids, live, counts, parent_of):
    devices = LEVELS * GROUP
    grid_rows = patches.reshape(devices, CAP, VARS, CELLS)
    grid_ids = patch_ids.reshape(devices, CAP)
    slot_index = jnp.arange(CAP, dtype=jnp.int32)
    held_count = live
    is_kept = slot_index[None, :] < held_count[:, None]
    grid_rows = jnp.where(is_kept[:, :, None, None], grid_rows, 0.0)
    grid_ids = jnp.where(is_kept, grid_ids, -1)
    members = np.arange(devices)
    for turn_index in range(ROUNDS):
        partner = (members // GROUP) * GROUP + ((members % GROUP) ^ (1 << turn_index))
        sent_count = counts[turn_index]
        out_rows, out_ids = jax.vmap(take_top)(grid_rows, grid_ids, held_count, sent_count)
        kept_count = held_count - sent_count
        grid_rows, grid_ids = jax.vmap(place_rows)(grid_rows, grid_ids, kept_count, out_rows[partner], out_ids[partner])
        held_count = kept_count + sent_count[partner]
    reduced = restrict(grid_rows).reshape(devices * CAP, VARS * COARSE)
    flat_ids = grid_ids.reshape(-1)
    parent = jnp.where(flat_ids >= 0, parent_of[jnp.clip(flat_ids, 0, SLOTS - 1)], PARENTS).astype(jnp.int32)
    coarse = jax.ops.segment_sum(reduced, parent, num_segments=PARENTS + 1)[:PARENTS]
    return grid_rows.reshape(SLOTS, VARS, CELLS), flat_ids, coarse.reshape(PARENTS, VARS, COARSE)
```

```python
import functools

import jax
import jax.numpy as jnp
from jax import lax
from jax.experimental import pallas as pl
from jax.experimental.pallas import tpu as pltpu
from jax.sharding import PartitionSpec as P

EDGE = 16
SEND_MOST = 4
PAR_DEV = 2
LANES = 128
ROWS = 8
MESH = pl.DeviceIdType.MESH


def pool_matrix():
    plane, half = EDGE * EDGE, EDGE // 2
    fine = lax.broadcasted_iota(jnp.int32, (2 * plane, half * half * 2), 0)
    coarse = lax.broadcasted_iota(jnp.int32, (2 * plane, half * half * 2), 1)
    same_z = (fine // plane) == (coarse // (half * half))
    same_y = ((fine % plane) // (2 * EDGE)) == ((coarse % (half * half)) // half)
    same_x = ((fine % EDGE) // 2) == (coarse % half)
    return jnp.where(same_z & same_y & same_x, 1.0, 0.0).astype(jnp.bfloat16)


def split(x):
    high = x.astype(jnp.bfloat16)
    low = (x - high.astype(jnp.float32)).astype(jnp.bfloat16)
    return high, low


def kernel(
    group, levels, rounds,
    x_ref, ids_ref, live_ref, counts_ref, parent_ref,
    out_ref, new_ids_ref, coarse_ref,
    work, result, out_rows, in_rows, out_marks, in_marks,
    part, part_in, held, held_in, gathered,
    read_sem, write_sem, row_send, row_recv, mark_send, mark_recv,
    a_send, a_recv, b_send, b_recv, c_send, c_recv,
):
    variables, capacity, cells = x_ref.shape
    first_rows = -(-(capacity - SEND_MOST * rounds) // ROWS) * ROWS
    tiles_per = gathered.shape[1]
    bal = lax.axis_index("bal")
    level = lax.axis_index("level")

    def partner(r):
        step = 1 << r
        return bal + step * (1 - 2 * ((bal // step) % 2))

    reads = [
        pltpu.make_async_copy(
            x_ref.at[v, pl.ds(0, first_rows)], work.at[v, pl.ds(0, first_rows)], read_sem.at[v]
        )
        for v in range(variables)
    ]
    for read in reads:
        read.start()

    barrier = pltpu.get_barrier_semaphore()
    for d in range(1, group):
        pl.semaphore_signal(barrier, inc=1, device_id={"bal": lax.rem(bal + d, group)}, device_id_type=MESH)
    for d in range(1, levels):
        pl.semaphore_signal(barrier, inc=1, device_id={"level": lax.rem(level + d, levels)}, device_id_type=MESH)

    lane = lax.broadcasted_iota(jnp.int32, (ROWS, LANES), 1)
    marks = jnp.full((ROWS, LANES), -1, jnp.int32)
    parent = jnp.full((ROWS, LANES), -1, jnp.int32)
    live = live_ref[0]
    known = parent_ref.shape[0] - 1
    for s in range(capacity):
        mark = ids_ref[s]
        marks = jnp.where(lane == s, mark, marks)
        if s < first_rows:
            parent = jnp.where(lane == s, parent_ref[jnp.clip(mark, 0, known)], parent)
    parent = jnp.where(lane < live, parent, -1)

    pl.semaphore_wait(barrier, group - 1 + levels - 1)

    width = 512
    half = cells // 2
    chunks = half // width
    row = lax.broadcasted_iota(jnp.int32, (ROWS, width), 0)

    def send_rows(r, v):
        return pltpu.make_async_remote_copy(
            src_ref=out_rows.at[r, v], dst_ref=in_rows.at[r, v],
            send_sem=row_send.at[r, v], recv_sem=row_recv.at[r, v],
            device_id={"bal": partner(r)}, device_id_type=MESH,
        )

    def send_marks(r):
        return pltpu.make_async_remote_copy(
            src_ref=out_marks.at[r], dst_ref=in_marks.at[r],
            send_sem=mark_send.at[r], recv_sem=mark_recv.at[r],
            device_id={"bal": partner(r)}, device_id_type=MESH,
        )

    def post_marks(r, marks, held_count, sent):
        start = held_count - sent
        moved = pltpu.roll(marks, lax.rem(LANES - start, LANES), 1)
        out_marks[r] = jnp.where(lane < sent, moved, -1)
        send_marks(r).start()

    def take_marks(r, marks, kept):
        send_marks(r).wait_recv()
        arrived = in_marks[r]
        count = jnp.sum(jnp.where(arrived[0:1] >= 0, 1, 0))
        moved = pltpu.roll(arrived, kept, 1)
        marks = jnp.where(lane < kept, marks, jnp.where(lane < kept + count, moved, -1))
        return marks, count

    def tile_count(r):
        return -(-(capacity - SEND_MOST * (rounds - r)) // ROWS)

    def pack(r, tiles_low, tiles_high, start, stop):
        def window(tiles, shift):
            picked = tiles[0]
            for t in range(1, len(tiles)):
                slot = row + t * ROWS
                picked = jnp.where((slot >= start) & (slot < stop), tiles[t], picked)
            return pltpu.roll(picked, shift, 0)

        back = lax.rem(8 * ROWS - start, ROWS)
        low = window(tiles_low, back)
        high = window(tiles_high, lax.rem(back + SEND_MOST, ROWS))
        return jnp.where(row < SEND_MOST, low, high)

    def load(v, t, lanes):
        return work[v, pl.ds(t * ROWS, ROWS), lanes]

    def lanes_of(c):
        low = pl.multiple_of(c * width, LANES)
        high = pl.multiple_of(half + c * width, LANES)
        return pl.ds(low, width), pl.ds(high, width)

    def merge(tiles, t_count, arrived, kept, count, is_high):
        shift = lax.rem(kept + (SEND_MOST if is_high else 0), ROWS)
        moved = pltpu.roll(arrived, shift, 0)
        merged = []
        for t in range(t_count):
            slot = row + t * ROWS
            fresh = jnp.where((slot >= kept) & (slot < kept + count), moved, 0.0)
            merged.append(jnp.where(slot < kept, tiles[t], fresh) if t < len(tiles) else fresh)
        return merged

    sent = counts_ref[0, 0]
    post_marks(0, marks, live, sent)
    for v in range(variables):
        reads[v].wait()

        def body(c, carry, v=v):
            low, high = lanes_of(c)
            count = tile_count(0)
            out_rows[0, v, :, low] = pack(
                0, [load(v, t, low) for t in range(count)],
                [load(v, t, high) for t in range(count)], live - sent, live,
            )
            return carry

        lax.fori_loop(0, chunks, body, 0)
        send_rows(0, v).start()

    pool = pool_matrix()
    parents = levels * PAR_DEV
    one_row = lax.broadcasted_iota(jnp.int32, (parents, first_rows), 0)
    one_hot = jnp.where(one_row == parent[0:1, :first_rows], 1.0, 0.0).astype(jnp.bfloat16)
    both_hot = jnp.concatenate([one_hot, one_hot], axis=1)
    plane = EDGE * EDGE
    quarters = cells // (4 * plane)
    slot_of = lax.broadcasted_iota(jnp.int32, (first_rows, plane), 0)
    for v in range(variables):
        rows = []
        for q in range(quarters):
            sums = []
            for k in (2 * q, 2 * q + 1):
                a = work[v, 0:first_rows, 2 * k * plane:(2 * k + 1) * plane]
                b = work[v, 0:first_rows, (2 * k + 1) * plane:(2 * k + 2) * plane]
                sums.append(jnp.where(slot_of < live, a + b, 0.0))
            rows.extend(split(jnp.concatenate(sums, axis=1)))
        pooled = jnp.dot(jnp.concatenate(rows, axis=0), pool, preferred_element_type=jnp.float32)
        for q in range(quarters):
            base = 2 * q * first_rows
            mean = 0.125 * (pooled[base:base + first_rows] + pooled[base + first_rows:base + 2 * first_rows])
            total = jnp.dot(
                both_hot, jnp.concatenate(split(mean), axis=0), preferred_element_type=jnp.float32
            )
            k = v * quarters + q
            for m in range(levels):
                part[k // tiles_per, m, k % tiles_per] = total[PAR_DEV * m:PAR_DEV * (m + 1)]
    for k in range(variables * quarters, group * tiles_per):
        part[k // tiles_per, :, k % tiles_per] = jnp.zeros((levels, PAR_DEV, LANES), jnp.float32)

    def send_a(d):
        to = lax.rem(bal + d, group)
        return pltpu.make_async_remote_copy(
            src_ref=part.at[to], dst_ref=part_in.at[d - 1],
            send_sem=a_send.at[d - 1], recv_sem=a_recv.at[d - 1],
            device_id={"bal": to}, device_id_type=MESH,
        )

    def send_b(d):
        to = lax.rem(level + d, levels)
        return pltpu.make_async_remote_copy(
            src_ref=held.at[to], dst_ref=held_in.at[d - 1],
            send_sem=b_send.at[d - 1], recv_sem=b_recv.at[d - 1],
            device_id={"level": to}, device_id_type=MESH,
        )

    def send_c(d):
        to = lax.rem(bal + d, group)
        return pltpu.make_async_remote_copy(
            src_ref=gathered.at[bal], dst_ref=gathered.at[bal],
            send_sem=c_send.at[d - 1], recv_sem=c_recv.at[d - 1],
            device_id={"bal": to}, device_id_type=MESH,
        )

    for d in range(1, group):
        send_a(d).start()

    held_count = live
    for r in range(1, rounds):
        kept = held_count - sent
        marks, count = take_marks(r - 1, marks, kept)
        held_count = kept + count
        sent = counts_ref[r, 0]
        post_marks(r, marks, held_count, sent)
        for v in range(variables):
            send_rows(r - 1, v).wait_recv()

            def body(c, carry, v=v, r=r, kept=kept, count=count, held_count=held_count, sent=sent):
                lanes = lanes_of(c)
                arrived = in_rows[r - 1, v, :, lanes[0]]
                merged = []
                for i in range(2):
                    tiles = [load(v, t, lanes[i]) for t in range(tile_count(r - 1))]
                    merged.append(merge(tiles, tile_count(r), arrived, kept, count, i == 1))
                    for t in range(tile_count(r)):
                        work[v, pl.ds(t * ROWS, ROWS), lanes[i]] = merged[i][t]
                out_rows[r, v, :, lanes[0]] = pack(
                    r, merged[0], merged[1], held_count - sent, held_count
                )
                return carry

            lax.fori_loop(0, chunks, body, 0)
            send_rows(r, v).start()

    for d in range(1, group):
        send_a(d).wait_recv()

    def add_a(m, carry):
        total = part[bal, m]
        for d in range(1, group):
            total = total + part_in[d - 1, m]
        held[m] = total
        return carry

    lax.fori_loop(0, levels, add_a, 0)
    for d in range(1, levels):
        send_b(d).start()
    for d in range(1, levels):
        send_b(d).wait_recv()
    total = held[level]
    for d in range(1, levels):
        total = total + held_in[d - 1]
    gathered[bal] = total
    for d in range(1, group):
        send_c(d).start()

    kept = held_count - sent
    marks, count = take_marks(rounds - 1, marks, kept)
    new_ids_ref[...] = marks[0:1]
    writes = []
    for v in range(variables):
        send_rows(rounds - 1, v).wait_recv()

        def body(c, carry, v=v):
            lanes = lanes_of(c)
            arrived = in_rows[rounds - 1, v, :, lanes[0]]
            for i in range(2):
                tiles = [load(v, t, lanes[i]) for t in range(tile_count(rounds - 1))]
                merged = merge(tiles, tile_count(rounds), arrived, kept, count, i == 1)
                for t in range(tile_count(rounds)):
                    size = min(ROWS, capacity - t * ROWS)
                    result[v, pl.ds(t * ROWS, size), lanes[i]] = merged[t][0:size]
            return carry

        lax.fori_loop(0, chunks, body, 0)
        writes.append(pltpu.make_async_copy(result.at[v], out_ref.at[v], write_sem.at[v]))
        writes[-1].start()

    for d in range(1, group):
        send_c(d).wait_recv()
    for k in range(variables * quarters):
        v, q = k // quarters, k % quarters
        coarse_ref[v, :, q * LANES:(q + 1) * LANES] = gathered[k // tiles_per, k % tiles_per]

    for r in range(rounds):
        send_marks(r).wait_send()
        for v in range(variables):
            send_rows(r, v).wait_send()
    for d in range(1, group):
        send_a(d).wait_send()
        send_c(d).wait_send()
    for d in range(1, levels):
        send_b(d).wait_send()
    for write in writes:
        write.wait()


def per_device(patches, patch_ids, live, counts, parent_of):
    capacity, variables, cells = patches.shape
    group = lax.axis_size("bal")
    levels = lax.axis_size("level")
    rounds = counts.shape[0]
    coarse_cells = cells // 8
    tiles_per = -(-(variables * coarse_cells // LANES) // group)
    padded = -(-capacity // ROWS) * ROWS
    f32 = jnp.float32
    dma = pltpu.SemaphoreType.DMA
    fine, ids, coarse = pl.pallas_call(
        functools.partial(kernel, group, levels, rounds),
        out_shape=(
            jax.ShapeDtypeStruct((variables, capacity, cells), f32),
            jax.ShapeDtypeStruct((1, LANES), jnp.int32),
            jax.ShapeDtypeStruct((variables, PAR_DEV, coarse_cells), f32),
        ),
        in_specs=[
            pl.BlockSpec(memory_space=pl.ANY),
            pl.BlockSpec(memory_space=pltpu.SMEM),
            pl.BlockSpec(memory_space=pltpu.SMEM),
            pl.BlockSpec(memory_space=pltpu.SMEM),
            pl.BlockSpec(memory_space=pltpu.SMEM),
        ],
        out_specs=(
            pl.BlockSpec(memory_space=pl.ANY),
            pl.BlockSpec(memory_space=pltpu.VMEM),
            pl.BlockSpec(memory_space=pltpu.VMEM),
        ),
        scratch_shapes=[
            pltpu.VMEM((variables, padded, cells), f32),
            pltpu.VMEM((variables, capacity, cells), f32),
            pltpu.VMEM((rounds, variables, ROWS, cells // 2), f32),
            pltpu.VMEM((rounds, variables, ROWS, cells // 2), f32),
            pltpu.VMEM((rounds, ROWS, LANES), jnp.int32),
            pltpu.VMEM((rounds, ROWS, LANES), jnp.int32),
            pltpu.VMEM((group, levels, tiles_per, PAR_DEV, LANES), f32),
            pltpu.VMEM((group - 1, levels, tiles_per, PAR_DEV, LANES), f32),
            pltpu.VMEM((levels, tiles_per, PAR_DEV, LANES), f32),
            pltpu.VMEM((levels - 1, tiles_per, PAR_DEV, LANES), f32),
            pltpu.VMEM((group, tiles_per, PAR_DEV, LANES), f32),
            dma((variables,)),
            dma((variables,)),
            dma((rounds, variables)),
            dma((rounds, variables)),
            dma((rounds,)),
            dma((rounds,)),
            dma((group - 1,)),
            dma((group - 1,)),
            dma((levels - 1,)),
            dma((levels - 1,)),
            dma((group - 1,)),
            dma((group - 1,)),
        ],
        compiler_params=pltpu.CompilerParams(collective_id=0, has_side_effects=True),
    )(patches.transpose(1, 0, 2), patch_ids, live, counts, parent_of)
    return (fine.transpose(1, 0, 2), ids[0, :capacity], coarse.transpose(1, 0, 2))


def solution(mesh):
    return jax.shard_map(
        per_device,
        mesh=mesh,
        in_specs=(
            P(("level", "bal"), None, None),
            P(("level", "bal")),
            P(("level", "bal")),
            P(None, ("level", "bal")),
            P(),
        ),
        out_specs=(P(("level", "bal"), None, None), P(("level", "bal")), P("level", None, None)),
        check_vma=False,
    )
```

```python
import functools

import jax
import jax.numpy as jnp
from jax import lax
from jax.experimental import pallas as pl
from jax.experimental.pallas import tpu as pltpu
from jax.sharding import PartitionSpec as P

EDGE = 16
SEND_MOST = 4
PAR_DEV = 2
LANES = 128
AHEAD = 2
ROWS = 8
MESH = pl.DeviceIdType.MESH


def pool_matrix():
    plane, half = EDGE * EDGE, EDGE // 2
    fine = lax.broadcasted_iota(jnp.int32, (2 * plane, half * half * 2), 0)
    coarse = lax.broadcasted_iota(jnp.int32, (2 * plane, half * half * 2), 1)
    same_z = (fine // plane) == (coarse // (half * half))
    same_y = ((fine % plane) // (2 * EDGE)) == ((coarse % (half * half)) // half)
    same_x = ((fine % EDGE) // 2) == (coarse % half)
    return jnp.where(same_z & same_y & same_x, 1.0, 0.0).astype(jnp.bfloat16)


def split(x):
    high = x.astype(jnp.bfloat16)
    low = (x - high.astype(jnp.float32)).astype(jnp.bfloat16)
    return high, low


def kernel(
    group, levels, rounds,
    x_ref, ids_ref, live_ref, counts_in, parent_ref,
    out_ref, new_ids_ref, coarse_ref,
    work, result, out_rows, in_rows, out_marks, in_marks,
    part, part_in, gathered, counts_ref, ids, parents_of,
    read_sem, small_sem, write_sem, row_send, row_recv, mark_send, mark_recv,
    a_send, a_recv, b_send, b_recv,
):
    variables, capacity, cells = x_ref.shape
    first_rows = -(-(capacity - SEND_MOST * rounds) // ROWS) * ROWS
    bal = lax.axis_index("bal")
    level = lax.axis_index("level")

    def partner(r):
        step = 1 << r
        return bal + step * (1 - 2 * ((bal // step) % 2))

    reads = [
        pltpu.make_async_copy(
            x_ref.at[v, pl.ds(0, first_rows)], work.at[0, v, pl.ds(0, first_rows)], read_sem.at[v]
        )
        for v in range(variables)
    ]
    small = [
        pltpu.make_async_copy(counts_in, counts_ref, small_sem.at[0]),
        pltpu.make_async_copy(ids_ref, ids, small_sem.at[1]),
        pltpu.make_async_copy(parent_ref, parents_of, small_sem.at[2]),
    ]
    for copy in small[:1] + reads[:1] + small[1:] + reads[1:]:
        copy.start()

    barrier = pltpu.get_barrier_semaphore()
    for d in range(1, group):
        pl.semaphore_signal(barrier, inc=1, device_id={"bal": lax.rem(bal + d, group)}, device_id_type=MESH)
    for d in range(1, levels):
        pl.semaphore_signal(barrier, inc=1, device_id={"level": lax.rem(level + d, levels)}, device_id_type=MESH)

    lane = lax.broadcasted_iota(jnp.int32, (ROWS, LANES), 1)
    small[0].wait()
    live = live_ref[0]
    width = 512
    half = cells // 2
    chunks = half // width
    row = lax.broadcasted_iota(jnp.int32, (ROWS, width), 0)

    def send_rows(r, v):
        return pltpu.make_async_remote_copy(
            src_ref=out_rows.at[r, v], dst_ref=in_rows.at[r, v],
            send_sem=row_send.at[r, v], recv_sem=row_recv.at[r, v],
            device_id={"bal": partner(r)}, device_id_type=MESH,
        )

    def send_marks(r):
        return pltpu.make_async_remote_copy(
            src_ref=out_marks.at[r], dst_ref=in_marks.at[r],
            send_sem=mark_send.at[r], recv_sem=mark_recv.at[r],
            device_id={"bal": partner(r)}, device_id_type=MESH,
        )

    def post_marks(r, marks, held_count, sent):
        start = held_count - sent
        moved = pltpu.roll(marks, lax.rem(LANES - start, LANES), 1)
        out_marks[r] = jnp.where(lane < sent, moved, -1)
        send_marks(r).start()

    def take_marks(r, marks, kept):
        send_marks(r).wait_recv()
        arrived = in_marks[r]
        count = jnp.sum(jnp.where(arrived[0:1] >= 0, 1, 0))
        moved = pltpu.roll(arrived, kept, 1)
        marks = jnp.where(lane < kept, marks, jnp.where(lane < kept + count, moved, -1))
        return marks, count

    def tile_count(r):
        return -(-(capacity - SEND_MOST * (rounds - r)) // ROWS)

    def pack(r, tiles_low, tiles_high, start, stop):
        def window(tiles, shift):
            picked = tiles[0]
            for t in range(1, len(tiles)):
                slot = row + t * ROWS
                picked = jnp.where((slot >= start) & (slot < stop), tiles[t], picked)
            return pltpu.roll(picked, shift, 0)

        back = lax.rem(8 * ROWS - start, ROWS)
        low = window(tiles_low, back)
        high = window(tiles_high, lax.rem(back + SEND_MOST, ROWS))
        return jnp.where(row < SEND_MOST, low, high)

    def load(r, v, t, lanes):
        return work[r, v, pl.ds(t * ROWS, ROWS), lanes]

    def lanes_of(c):
        low = pl.multiple_of(c * width, LANES)
        high = pl.multiple_of(half + c * width, LANES)
        return pl.ds(low, width), pl.ds(high, width)

    def merge(tiles, t_count, arrived, kept, count, is_high):
        shift = lax.rem(kept + (SEND_MOST if is_high else 0), ROWS)
        moved = pltpu.roll(arrived, shift, 0)
        merged = []
        for t in range(t_count):
            slot = row + t * ROWS
            fresh = jnp.where((slot >= kept) & (slot < kept + count), moved, 0.0)
            merged.append(jnp.where(slot < kept, tiles[t], fresh) if t < len(tiles) else fresh)
        return merged

    sent = counts_ref[0]
    for v in range(variables):
        reads[v].wait()

        def body(c, carry, v=v):
            low, high = lanes_of(c)
            count = tile_count(0)
            out_rows[0, v, :, low] = pack(
                0, [load(0, v, t, low) for t in range(count)],
                [load(0, v, t, high) for t in range(count)], live - sent, live,
            )
            return carry

        lax.fori_loop(0, chunks, body, 0)
        if v == 0:
            pl.semaphore_wait(barrier, group - 1 + levels - 1)
        send_rows(0, v).start()
        if v == 0:
            for copy in small[1:]:
                copy.wait()
            marks = jnp.full((ROWS, LANES), -1, jnp.int32)
            for s in range(capacity):
                marks = jnp.where(lane == s, ids[s], marks)
            post_marks(0, marks, live, sent)

    parent = jnp.full((ROWS, LANES), -1, jnp.int32)
    for s in range(first_rows):
        mine = parents_of[jnp.clip(ids[s], 0, parents_of.shape[0] - 1)]
        parent = jnp.where(lane == s, mine, parent)
    parent = jnp.where(lane < live, parent, -1)

    pool = pool_matrix()
    parents = levels * PAR_DEV
    one_row = lax.broadcasted_iota(jnp.int32, (parents, first_rows), 0)
    one_hot = jnp.where(one_row == parent[0:1, :first_rows], 1.0, 0.0).astype(jnp.bfloat16)
    both_hot = jnp.concatenate([one_hot, one_hot], axis=1)
    plane = EDGE * EDGE
    quarters = cells // (4 * plane)
    slot_of = lax.broadcasted_iota(jnp.int32, (first_rows, plane), 0)
    def restrict_rows(v):
        rows = []
        for q in range(quarters):
            sums = []
            for k in (2 * q, 2 * q + 1):
                a = work[0, v, 0:first_rows, 2 * k * plane:(2 * k + 1) * plane]
                b = work[0, v, 0:first_rows, (2 * k + 1) * plane:(2 * k + 2) * plane]
                sums.append(jnp.where(slot_of < live, a + b, 0.0))
            rows.extend(split(jnp.concatenate(sums, axis=1)))
        pooled = jnp.dot(jnp.concatenate(rows, axis=0), pool, preferred_element_type=jnp.float32)
        for q in range(quarters):
            base = 2 * q * first_rows
            mean = 0.125 * (pooled[base:base + first_rows] + pooled[base + first_rows:base + 2 * first_rows])
            total = jnp.dot(
                both_hot, jnp.concatenate(split(mean), axis=0), preferred_element_type=jnp.float32
            )
            for m in range(levels):
                part[m, v, :, q * LANES:(q + 1) * LANES] = total[PAR_DEV * m:PAR_DEV * (m + 1)]


    def send_a(d):
        to = lax.rem(level + d, levels)
        return pltpu.make_async_remote_copy(
            src_ref=part.at[to], dst_ref=part_in.at[d - 1],
            send_sem=a_send.at[d - 1], recv_sem=a_recv.at[d - 1],
            device_id={"level": to}, device_id_type=MESH,
        )

    def send_b(d):
        to = lax.rem(bal + d, group)
        return pltpu.make_async_remote_copy(
            src_ref=gathered.at[bal], dst_ref=gathered.at[bal],
            send_sem=b_send.at[d - 1], recv_sem=b_recv.at[d - 1],
            device_id={"bal": to}, device_id_type=MESH,
        )

    def parent_sums():
        for v in range(variables):
            restrict_rows(v)
        for d in range(1, levels):
            send_a(d).start()

    held_count = live
    for r in range(1, rounds):
        kept = held_count - sent
        marks, count = take_marks(r - 1, marks, kept)
        held_count = kept + count
        sent = counts_ref[r]
        post_marks(r, marks, held_count, sent)
        for v in range(variables):
            if r == 1 and v == AHEAD:
                parent_sums()
            send_rows(r - 1, v).wait_recv()

            def body(c, carry, v=v, r=r, kept=kept, count=count, held_count=held_count, sent=sent):
                lanes = lanes_of(c)
                arrived = in_rows[r - 1, v, :, lanes[0]]
                merged = []
                for i in range(2):
                    tiles = [load(r - 1, v, t, lanes[i]) for t in range(tile_count(r - 1))]
                    merged.append(merge(tiles, tile_count(r), arrived, kept, count, i == 1))
                    for t in range(tile_count(r)):
                        work[r, v, pl.ds(t * ROWS, ROWS), lanes[i]] = merged[i][t]
                out_rows[r, v, :, lanes[0]] = pack(
                    r, merged[0], merged[1], held_count - sent, held_count
                )
                return carry

            lax.fori_loop(0, chunks, body, 0)
            send_rows(r, v).start()

    for d in range(1, levels):
        send_a(d).wait_recv()
    total = part[level]
    for d in range(1, levels):
        total = total + part_in[d - 1]
    gathered[bal] = total
    for d in range(1, group):
        send_b(d).start()

    kept = held_count - sent
    marks, count = take_marks(rounds - 1, marks, kept)
    new_ids_ref[...] = marks[0:1]
    writes = []
    for v in range(variables):
        send_rows(rounds - 1, v).wait_recv()

        def body(c, carry, v=v):
            lanes = lanes_of(c)
            arrived = in_rows[rounds - 1, v, :, lanes[0]]
            for i in range(2):
                tiles = [load(rounds - 1, v, t, lanes[i]) for t in range(tile_count(rounds - 1))]
                merged = merge(tiles, tile_count(rounds), arrived, kept, count, i == 1)
                for t in range(tile_count(rounds)):
                    size = min(ROWS, capacity - t * ROWS)
                    result[v, pl.ds(t * ROWS, size), lanes[i]] = merged[t][0:size]
            return carry

        lax.fori_loop(0, chunks, body, 0)
        writes.append(pltpu.make_async_copy(result.at[v], out_ref.at[v], write_sem.at[v]))
        writes[-1].start()

    for d in range(1, group):
        send_b(d).wait_recv()
    total = gathered[0]
    for b in range(1, group):
        total = total + gathered[b]
    coarse_ref[...] = total

    for r in range(rounds):
        send_marks(r).wait_send()
        for v in range(variables):
            send_rows(r, v).wait_send()
    for d in range(1, group):
        send_b(d).wait_send()
    for d in range(1, levels):
        send_a(d).wait_send()
    for write in writes:
        write.wait()


def hbm(x):
    return pltpu.with_memory_space_constraint(x, pltpu.HBM)


def per_device(patches, patch_ids, live, counts, parent_of):
    capacity, variables, cells = patches.shape
    group = lax.axis_size("bal")
    levels = lax.axis_size("level")
    rounds = counts.shape[0]
    coarse_cells = cells // 8
    padded = -(-capacity // ROWS) * ROWS
    f32 = jnp.float32
    dma = pltpu.SemaphoreType.DMA
    fine, ids, coarse = pl.pallas_call(
        functools.partial(kernel, group, levels, rounds),
        out_shape=(
            jax.ShapeDtypeStruct((variables, capacity, cells), f32),
            jax.ShapeDtypeStruct((1, LANES), jnp.int32),
            jax.ShapeDtypeStruct((variables, PAR_DEV, coarse_cells), f32),
        ),
        in_specs=[
            pl.BlockSpec(memory_space=pltpu.HBM),
            pl.BlockSpec(memory_space=pltpu.HBM),
            pl.BlockSpec(memory_space=pltpu.SMEM),
            pl.BlockSpec(memory_space=pltpu.HBM),
            pl.BlockSpec(memory_space=pltpu.HBM),
        ],
        out_specs=(
            pl.BlockSpec(memory_space=pl.ANY),
            pl.BlockSpec(memory_space=pltpu.VMEM),
            pl.BlockSpec(memory_space=pltpu.VMEM),
        ),
        scratch_shapes=[
            pltpu.VMEM((rounds, variables, padded, cells), f32),
            pltpu.VMEM((variables, capacity, cells), f32),
            pltpu.VMEM((rounds, variables, ROWS, cells // 2), f32),
            pltpu.VMEM((rounds, variables, ROWS, cells // 2), f32),
            pltpu.VMEM((rounds, ROWS, LANES), jnp.int32),
            pltpu.VMEM((rounds, ROWS, LANES), jnp.int32),
            pltpu.VMEM((levels, variables, PAR_DEV, coarse_cells), f32),
            pltpu.VMEM((levels - 1, variables, PAR_DEV, coarse_cells), f32),
            pltpu.VMEM((group, variables, PAR_DEV, coarse_cells), f32),
            pltpu.SMEM((rounds,), jnp.int32),
            pltpu.SMEM(patch_ids.shape, jnp.int32),
            pltpu.SMEM(parent_of.shape, jnp.int32),
            dma((variables,)),
            dma((3,)),
            dma((variables,)),
            dma((rounds, variables)),
            dma((rounds, variables)),
            dma((rounds,)),
            dma((rounds,)),
            dma((levels - 1,)),
            dma((levels - 1,)),
            dma((group - 1,)),
            dma((group - 1,)),
        ],
        compiler_params=pltpu.CompilerParams(collective_id=0, has_side_effects=True, vmem_limit_bytes=24 << 20),
    )(hbm(patches.transpose(1, 0, 2)), hbm(patch_ids), live, hbm(counts.reshape(rounds)), hbm(parent_of))
    return (fine.transpose(1, 0, 2), ids[0, :capacity], coarse.transpose(1, 0, 2))


def solution(mesh):
    return jax.shard_map(
        per_device,
        mesh=mesh,
        in_specs=(
            P(("level", "bal"), None, None),
            P(("level", "bal")),
            P(("level", "bal")),
            P(None, ("level", "bal")),
            P(),
        ),
        out_specs=(P(("level", "bal"), None, None), P(("level", "bal")), P("level", None, None)),
        check_vma=False,
    )
```

```python
import functools

import jax
import jax.numpy as jnp
from jax import lax
from jax.experimental import pallas as pl
from jax.experimental.pallas import tpu as pltpu
from jax.sharding import PartitionSpec as P

EDGE = 16
SEND_MOST = 4
PAR_DEV = 2
LANES = 128
AHEAD = 2
ROWS = 8
MESH = pl.DeviceIdType.MESH


def pool_matrix():
    plane, half = EDGE * EDGE, EDGE // 2
    fine = lax.broadcasted_iota(jnp.int32, (2 * plane, half * half * 2), 0)
    coarse = lax.broadcasted_iota(jnp.int32, (2 * plane, half * half * 2), 1)
    same_z = (fine // plane) == (coarse // (half * half))
    same_y = ((fine % plane) // (2 * EDGE)) == ((coarse % (half * half)) // half)
    same_x = ((fine % EDGE) // 2) == (coarse % half)
    return jnp.where(same_z & same_y & same_x, 1.0, 0.0).astype(jnp.bfloat16)


def split(x):
    high = x.astype(jnp.bfloat16)
    low = (x - high.astype(jnp.float32)).astype(jnp.bfloat16)
    return high, low


def kernel(
    group, levels, rounds,
    x_ref, ids_ref, live_ref, counts_in, parent_ref,
    out_ref, new_ids_ref, coarse_ref,
    work, out_rows, in_rows, out_marks, in_marks,
    part, part_in, gathered, counts_ref, ids, parents_of,
    read_sem, small_sem, row_send, row_recv, mark_send, mark_recv,
    a_send, a_recv, b_send, b_recv,
):
    variables, capacity, cells = x_ref.shape
    first_rows = -(-(capacity - SEND_MOST * rounds) // ROWS) * ROWS
    bal = lax.axis_index("bal")
    level = lax.axis_index("level")

    def partner(r):
        step = 1 << r
        return bal + step * (1 - 2 * ((bal // step) % 2))

    reads = [
        pltpu.make_async_copy(
            x_ref.at[v, pl.ds(0, first_rows)], work.at[0, v, pl.ds(0, first_rows)], read_sem.at[v]
        )
        for v in range(variables)
    ]
    small = [
        pltpu.make_async_copy(counts_in, counts_ref, small_sem.at[0]),
        pltpu.make_async_copy(ids_ref, ids, small_sem.at[1]),
        pltpu.make_async_copy(parent_ref, parents_of, small_sem.at[2]),
    ]
    for copy in small[:1] + reads[:1] + small[1:] + reads[1:]:
        copy.start()

    barrier = pltpu.get_barrier_semaphore()
    for d in range(1, group):
        pl.semaphore_signal(barrier, inc=1, device_id={"bal": lax.rem(bal + d, group)}, device_id_type=MESH)
    for d in range(1, levels):
        pl.semaphore_signal(barrier, inc=1, device_id={"level": lax.rem(level + d, levels)}, device_id_type=MESH)

    lane = lax.broadcasted_iota(jnp.int32, (ROWS, LANES), 1)
    small[0].wait()
    live = live_ref[0]
    width = 512
    half = cells // 2
    chunks = half // width
    row = lax.broadcasted_iota(jnp.int32, (ROWS, width), 0)

    def send_rows(r, v):
        return pltpu.make_async_remote_copy(
            src_ref=out_rows.at[r, v], dst_ref=in_rows.at[r, v],
            send_sem=row_send.at[r, v], recv_sem=row_recv.at[r, v],
            device_id={"bal": partner(r)}, device_id_type=MESH,
        )

    def send_marks(r):
        return pltpu.make_async_remote_copy(
            src_ref=out_marks.at[r], dst_ref=in_marks.at[r],
            send_sem=mark_send.at[r], recv_sem=mark_recv.at[r],
            device_id={"bal": partner(r)}, device_id_type=MESH,
        )

    def post_marks(r, marks, held_count, sent):
        start = held_count - sent
        moved = pltpu.roll(marks, lax.rem(LANES - start, LANES), 1)
        out_marks[r] = jnp.where(lane < sent, moved, -1)
        send_marks(r).start()

    def take_marks(r, marks, kept):
        send_marks(r).wait_recv()
        arrived = in_marks[r]
        count = jnp.sum(jnp.where(arrived[0:1] >= 0, 1, 0))
        moved = pltpu.roll(arrived, kept, 1)
        marks = jnp.where(lane < kept, marks, jnp.where(lane < kept + count, moved, -1))
        return marks, count

    def tile_count(r):
        return -(-(capacity - SEND_MOST * (rounds - r)) // ROWS)

    def pack(r, tiles_low, tiles_high, start, stop):
        def window(tiles, shift):
            picked = tiles[0]
            for t in range(1, len(tiles)):
                slot = row + t * ROWS
                picked = jnp.where((slot >= start) & (slot < stop), tiles[t], picked)
            return pltpu.roll(picked, shift, 0)

        back = lax.rem(8 * ROWS - start, ROWS)
        low = window(tiles_low, back)
        high = window(tiles_high, lax.rem(back + SEND_MOST, ROWS))
        return jnp.where(row < SEND_MOST, low, high)

    def load(r, v, t, lanes):
        return work[r, v, pl.ds(t * ROWS, ROWS), lanes]

    def lanes_of(c):
        low = pl.multiple_of(c * width, LANES)
        high = pl.multiple_of(half + c * width, LANES)
        return pl.ds(low, width), pl.ds(high, width)

    def merge(tiles, t_count, arrived, kept, count, is_high):
        shift = lax.rem(kept + (SEND_MOST if is_high else 0), ROWS)
        moved = pltpu.roll(arrived, shift, 0)
        merged = []
        for t in range(t_count):
            slot = row + t * ROWS
            fresh = jnp.where((slot >= kept) & (slot < kept + count), moved, 0.0)
            merged.append(jnp.where(slot < kept, tiles[t], fresh) if t < len(tiles) else fresh)
        return merged

    sent = counts_ref[0]
    for v in range(variables):
        reads[v].wait()

        def body(c, carry, v=v):
            low, high = lanes_of(c)
            count = tile_count(0)
            out_rows[0, v, :, low] = pack(
                0, [load(0, v, t, low) for t in range(count)],
                [load(0, v, t, high) for t in range(count)], live - sent, live,
            )
            return carry

        lax.fori_loop(0, chunks, body, 0)
        if v == 0:
            pl.semaphore_wait(barrier, group - 1 + levels - 1)
        send_rows(0, v).start()
        if v == 0:
            for copy in small[1:]:
                copy.wait()
            marks = jnp.full((ROWS, LANES), -1, jnp.int32)
            for s in range(capacity):
                marks = jnp.where(lane == s, ids[s], marks)
            post_marks(0, marks, live, sent)

    parent = jnp.full((ROWS, LANES), -1, jnp.int32)
    for s in range(first_rows):
        mine = parents_of[jnp.clip(ids[s], 0, parents_of.shape[0] - 1)]
        parent = jnp.where(lane == s, mine, parent)
    parent = jnp.where(lane < live, parent, -1)

    pool = pool_matrix()
    parents = levels * PAR_DEV
    one_row = lax.broadcasted_iota(jnp.int32, (parents, first_rows), 0)
    one_hot = jnp.where(one_row == parent[0:1, :first_rows], 1.0, 0.0).astype(jnp.bfloat16)
    both_hot = jnp.concatenate([one_hot, one_hot], axis=1)
    plane = EDGE * EDGE
    quarters = cells // (4 * plane)
    slot_of = lax.broadcasted_iota(jnp.int32, (first_rows, plane), 0)
    def restrict_rows(v):
        rows = []
        for q in range(quarters):
            sums = []
            for k in (2 * q, 2 * q + 1):
                a = work[0, v, 0:first_rows, 2 * k * plane:(2 * k + 1) * plane]
                b = work[0, v, 0:first_rows, (2 * k + 1) * plane:(2 * k + 2) * plane]
                sums.append(jnp.where(slot_of < live, a + b, 0.0))
            rows.extend(split(jnp.concatenate(sums, axis=1)))
        pooled = jnp.dot(jnp.concatenate(rows, axis=0), pool, preferred_element_type=jnp.float32)
        for q in range(quarters):
            base = 2 * q * first_rows
            mean = 0.125 * (pooled[base:base + first_rows] + pooled[base + first_rows:base + 2 * first_rows])
            total = jnp.dot(
                both_hot, jnp.concatenate(split(mean), axis=0), preferred_element_type=jnp.float32
            )
            for m in range(levels):
                part[m, v, :, q * LANES:(q + 1) * LANES] = total[PAR_DEV * m:PAR_DEV * (m + 1)]


    def send_a(d):
        to = lax.rem(level + d, levels)
        return pltpu.make_async_remote_copy(
            src_ref=part.at[to], dst_ref=part_in.at[d - 1],
            send_sem=a_send.at[d - 1], recv_sem=a_recv.at[d - 1],
            device_id={"level": to}, device_id_type=MESH,
        )

    def send_b(d):
        to = lax.rem(bal + d, group)
        return pltpu.make_async_remote_copy(
            src_ref=gathered.at[bal], dst_ref=gathered.at[bal],
            send_sem=b_send.at[d - 1], recv_sem=b_recv.at[d - 1],
            device_id={"bal": to}, device_id_type=MESH,
        )

    def parent_sums():
        for v in range(variables):
            restrict_rows(v)
        for d in range(1, levels):
            send_a(d).start()

    held_count = live
    for r in range(1, rounds):
        kept = held_count - sent
        marks, count = take_marks(r - 1, marks, kept)
        held_count = kept + count
        sent = counts_ref[r]
        post_marks(r, marks, held_count, sent)
        for v in range(variables):
            if r == 1 and v == AHEAD:
                parent_sums()
            send_rows(r - 1, v).wait_recv()

            def body(c, carry, v=v, r=r, kept=kept, count=count, held_count=held_count, sent=sent):
                lanes = lanes_of(c)
                arrived = in_rows[r - 1, v, :, lanes[0]]
                merged = []
                for i in range(2):
                    tiles = [load(r - 1, v, t, lanes[i]) for t in range(tile_count(r - 1))]
                    merged.append(merge(tiles, tile_count(r), arrived, kept, count, i == 1))
                    for t in range(tile_count(r)):
                        work[r, v, pl.ds(t * ROWS, ROWS), lanes[i]] = merged[i][t]
                out_rows[r, v, :, lanes[0]] = pack(
                    r, merged[0], merged[1], held_count - sent, held_count
                )
                return carry

            lax.fori_loop(0, chunks, body, 0)
            send_rows(r, v).start()

    for d in range(1, levels):
        send_a(d).wait_recv()
    total = part[level]
    for d in range(1, levels):
        total = total + part_in[d - 1]
    gathered[bal] = total
    for d in range(1, group):
        send_b(d).start()

    kept = held_count - sent
    marks, count = take_marks(rounds - 1, marks, kept)
    new_ids_ref[...] = marks[0:1]
    for v in range(variables):
        send_rows(rounds - 1, v).wait_recv()

        def body(c, carry, v=v):
            lanes = lanes_of(c)
            arrived = in_rows[rounds - 1, v, :, lanes[0]]
            for i in range(2):
                tiles = [load(rounds - 1, v, t, lanes[i]) for t in range(tile_count(rounds - 1))]
                merged = merge(tiles, tile_count(rounds), arrived, kept, count, i == 1)
                for t in range(tile_count(rounds)):
                    size = min(ROWS, capacity - t * ROWS)
                    out_ref[v, pl.ds(t * ROWS, size), lanes[i]] = merged[t][0:size]
            return carry

        lax.fori_loop(0, chunks, body, 0)

    for d in range(1, group):
        send_b(d).wait_recv()
    total = gathered[0]
    for b in range(1, group):
        total = total + gathered[b]
    coarse_ref[...] = total

    for r in range(rounds):
        send_marks(r).wait_send()
        for v in range(variables):
            send_rows(r, v).wait_send()
    for d in range(1, group):
        send_b(d).wait_send()
    for d in range(1, levels):
        send_a(d).wait_send()


def finish(fine_ref, marks_ref, sums_ref, out_ref, ids_ref, coarse_ref, sem):
    variables = fine_ref.shape[0]
    copies = [
        pltpu.make_async_copy(fine_ref.at[v], out_ref.at[v], sem.at[v]) for v in range(variables)
    ]
    copies.append(pltpu.make_async_copy(sums_ref, coarse_ref, sem.at[variables]))
    for copy in copies:
        copy.start()
    ids_ref[...] = marks_ref[0, :ids_ref.shape[0]]
    for copy in copies:
        copy.wait()


def hbm(x):
    return pltpu.with_memory_space_constraint(x, pltpu.HBM)


def per_device(patches, patch_ids, live, counts, parent_of):
    capacity, variables, cells = patches.shape
    group = lax.axis_size("bal")
    levels = lax.axis_size("level")
    rounds = counts.shape[0]
    coarse_cells = cells // 8
    padded = -(-capacity // ROWS) * ROWS
    f32 = jnp.float32
    dma = pltpu.SemaphoreType.DMA
    fine, ids, coarse = pl.pallas_call(
        functools.partial(kernel, group, levels, rounds),
        out_shape=(
            jax.ShapeDtypeStruct((variables, capacity, cells), f32),
            jax.ShapeDtypeStruct((1, LANES), jnp.int32),
            jax.ShapeDtypeStruct((variables, PAR_DEV, coarse_cells), f32),
        ),
        in_specs=[
            pl.BlockSpec(memory_space=pltpu.HBM),
            pl.BlockSpec(memory_space=pltpu.HBM),
            pl.BlockSpec(memory_space=pltpu.SMEM),
            pl.BlockSpec(memory_space=pltpu.HBM),
            pl.BlockSpec(memory_space=pltpu.HBM),
        ],
        out_specs=(
            pl.BlockSpec(memory_space=pltpu.VMEM),
            pl.BlockSpec(memory_space=pltpu.VMEM),
            pl.BlockSpec(memory_space=pltpu.VMEM),
        ),
        scratch_shapes=[
            pltpu.VMEM((rounds, variables, padded, cells), f32),
            pltpu.VMEM((rounds, variables, ROWS, cells // 2), f32),
            pltpu.VMEM((rounds, variables, ROWS, cells // 2), f32),
            pltpu.VMEM((rounds, ROWS, LANES), jnp.int32),
            pltpu.VMEM((rounds, ROWS, LANES), jnp.int32),
            pltpu.VMEM((levels, variables, PAR_DEV, coarse_cells), f32),
            pltpu.VMEM((levels - 1, variables, PAR_DEV, coarse_cells), f32),
            pltpu.VMEM((group, variables, PAR_DEV, coarse_cells), f32),
            pltpu.SMEM((rounds,), jnp.int32),
            pltpu.SMEM(patch_ids.shape, jnp.int32),
            pltpu.SMEM(parent_of.shape, jnp.int32),
            dma((variables,)),
            dma((3,)),
            dma((rounds, variables)),
            dma((rounds, variables)),
            dma((rounds,)),
            dma((rounds,)),
            dma((levels - 1,)),
            dma((levels - 1,)),
            dma((group - 1,)),
            dma((group - 1,)),
        ],
        compiler_params=pltpu.CompilerParams(collective_id=0, has_side_effects=True, vmem_limit_bytes=24 << 20),
    )(hbm(patches.transpose(1, 0, 2)), hbm(patch_ids), live, hbm(counts.reshape(rounds)), hbm(parent_of))
    fine, ids, coarse = pl.pallas_call(
        finish,
        out_shape=(
            jax.ShapeDtypeStruct(fine.shape, f32),
            jax.ShapeDtypeStruct((capacity,), jnp.int32),
            jax.ShapeDtypeStruct(coarse.shape, f32),
        ),
        in_specs=[
            pl.BlockSpec(memory_space=pl.ANY),
            pl.BlockSpec(memory_space=pltpu.VMEM),
            pl.BlockSpec(memory_space=pl.ANY),
        ],
        out_specs=(
            pl.BlockSpec(memory_space=pl.ANY),
            pl.BlockSpec(memory_space=pltpu.VMEM),
            pl.BlockSpec(memory_space=pl.ANY),
        ),
        scratch_shapes=[dma((variables + 1,))],
        compiler_params=pltpu.CompilerParams(vmem_limit_bytes=24 << 20),
    )(fine, ids, coarse)
    return (fine.transpose(1, 0, 2), ids, coarse.transpose(1, 0, 2))


def solution(mesh):
    return jax.shard_map(
        per_device,
        mesh=mesh,
        in_specs=(
            P(("level", "bal"), None, None),
            P(("level", "bal")),
            P(("level", "bal")),
            P(None, ("level", "bal")),
            P(),
        ),
        out_specs=(P(("level", "bal"), None, None), P(("level", "bal")), P("level", None, None)),
        check_vma=False,
    )
```

```python
import functools

import jax
import jax.numpy as jnp
from jax import lax
from jax.experimental import pallas as pl
from jax.experimental.pallas import tpu as pltpu
from jax.sharding import PartitionSpec as P

EDGE = 16
SEND_MOST = 4
PAR_DEV = 2
LANES = 128
AHEAD = 0
SUMS_AT = 2
ROWS = 8
MESH = pl.DeviceIdType.MESH


def pool_matrix():
    plane, half = EDGE * EDGE, EDGE // 2
    fine = lax.broadcasted_iota(jnp.int32, (2 * plane, half * half * 2), 0)
    coarse = lax.broadcasted_iota(jnp.int32, (2 * plane, half * half * 2), 1)
    same_z = (fine // plane) == (coarse // (half * half))
    same_y = ((fine % plane) // (2 * EDGE)) == ((coarse % (half * half)) // half)
    same_x = ((fine % EDGE) // 2) == (coarse % half)
    return jnp.where(same_z & same_y & same_x, 1.0, 0.0).astype(jnp.bfloat16)


def split(x):
    high = x.astype(jnp.bfloat16)
    low = (x - high.astype(jnp.float32)).astype(jnp.bfloat16)
    return high, low


def kernel(
    group, levels, rounds,
    x_ref, ids_ref, live_ref, counts_in, parent_ref,
    out_ref, new_ids_ref, coarse_ref,
    work, out_rows, in_rows, out_marks, in_marks,
    part, part_in, gathered, counts_ref, ids, parents_of,
    read_sem, small_sem, row_send, row_recv, mark_send, mark_recv,
    a_send, a_recv, b_send, b_recv, ready, go,
):
    variables, capacity, cells = x_ref.shape
    first_rows = -(-(capacity - SEND_MOST * rounds) // ROWS) * ROWS
    bal = lax.axis_index("bal")
    level = lax.axis_index("level")

    def partner(r):
        step = 1 << r
        return bal + step * (1 - 2 * ((bal // step) % 2))

    reads = [
        pltpu.make_async_copy(
            x_ref.at[v, pl.ds(0, first_rows)], work.at[0, v, pl.ds(0, first_rows)], read_sem.at[v]
        )
        for v in range(variables)
    ]
    small = [
        pltpu.make_async_copy(counts_in, counts_ref, small_sem.at[0]),
        pltpu.make_async_copy(ids_ref, ids, small_sem.at[1]),
        pltpu.make_async_copy(parent_ref, parents_of, small_sem.at[2]),
    ]
    for copy in small[:1] + reads[:1] + small[1:] + reads[1:]:
        copy.start()

    barrier = pltpu.get_barrier_semaphore()
    hub = group - 1
    for d in range(1, group):
        to = lax.rem(bal + d, group)

        @pl.when(to != hub)
        def _(to=to):
            pl.semaphore_signal(barrier, inc=1, device_id={"bal": to}, device_id_type=MESH)

    lane = lax.broadcasted_iota(jnp.int32, (ROWS, LANES), 1)
    small[0].wait()
    live = live_ref[0]
    width = 512
    half = cells // 2
    chunks = half // width
    row = lax.broadcasted_iota(jnp.int32, (ROWS, width), 0)

    def send_rows(r, v):
        return pltpu.make_async_remote_copy(
            src_ref=out_rows.at[r, v], dst_ref=in_rows.at[r, v],
            send_sem=row_send.at[r, v], recv_sem=row_recv.at[r, v],
            device_id={"bal": partner(r)}, device_id_type=MESH,
        )

    def send_marks(r):
        return pltpu.make_async_remote_copy(
            src_ref=out_marks.at[r], dst_ref=in_marks.at[r],
            send_sem=mark_send.at[r], recv_sem=mark_recv.at[r],
            device_id={"bal": partner(r)}, device_id_type=MESH,
        )

    def post_marks(r, marks, held_count, sent):
        start = held_count - sent
        moved = pltpu.roll(marks, lax.rem(LANES - start, LANES), 1)
        out_marks[r] = jnp.where(lane < sent, moved, -1)
        send_marks(r).start()

    def take_marks(r, marks, kept):
        send_marks(r).wait_recv()
        arrived = in_marks[r]
        count = jnp.sum(jnp.where(arrived[0:1] >= 0, 1, 0))
        moved = pltpu.roll(arrived, kept, 1)
        marks = jnp.where(lane < kept, marks, jnp.where(lane < kept + count, moved, -1))
        return marks, count

    def tile_count(r):
        return -(-(capacity - SEND_MOST * (rounds - r)) // ROWS)

    def pack(r, tiles_low, tiles_high, start, stop):
        def window(tiles, shift):
            picked = tiles[0]
            for t in range(1, len(tiles)):
                slot = row + t * ROWS
                picked = jnp.where((slot >= start) & (slot < stop), tiles[t], picked)
            return pltpu.roll(picked, shift, 0)

        back = lax.rem(8 * ROWS - start, ROWS)
        low = window(tiles_low, back)
        high = window(tiles_high, lax.rem(back + SEND_MOST, ROWS))
        return jnp.where(row < SEND_MOST, low, high)

    def load(r, v, t, lanes):
        return work[r, v, pl.ds(t * ROWS, ROWS), lanes]

    def lanes_of(c):
        low = pl.multiple_of(c * width, LANES)
        high = pl.multiple_of(half + c * width, LANES)
        return pl.ds(low, width), pl.ds(high, width)

    def merge(tiles, t_count, arrived, kept, count, is_high):
        shift = lax.rem(kept + (SEND_MOST if is_high else 0), ROWS)
        moved = pltpu.roll(arrived, shift, 0)
        merged = []
        for t in range(t_count):
            slot = row + t * ROWS
            fresh = jnp.where((slot >= kept) & (slot < kept + count), moved, 0.0)
            merged.append(jnp.where(slot < kept, tiles[t], fresh) if t < len(tiles) else fresh)
        return merged

    def enter():
        @pl.when(bal != hub)
        def _():
            pl.semaphore_wait(barrier, group - 1)
            pl.semaphore_signal(ready, inc=1, device_id={"bal": hub}, device_id_type=MESH)

        @pl.when(bal == hub)
        def _():
            pl.semaphore_wait(ready, group - 1)
            for d in range(1, levels):
                to = lax.rem(level + d, levels)
                pl.semaphore_signal(barrier, inc=1, device_id={"level": to}, device_id_type=MESH)

    def enter_levels():
        @pl.when(bal == hub)
        def _():
            pl.semaphore_wait(barrier, levels - 1)
            for d in range(1, group):
                to = lax.rem(bal + d, group)
                pl.semaphore_signal(go, inc=1, device_id={"bal": to}, device_id_type=MESH)

        @pl.when(bal != hub)
        def _():
            pl.semaphore_wait(go, 1)

    sent = counts_ref[0]
    for v in range(variables):
        reads[v].wait()

        def body(c, carry, v=v):
            low, high = lanes_of(c)
            count = tile_count(0)
            out_rows[0, v, :, low] = pack(
                0, [load(0, v, t, low) for t in range(count)],
                [load(0, v, t, high) for t in range(count)], live - sent, live,
            )
            return carry

        lax.fori_loop(0, chunks, body, 0)
        if v == 0:
            enter()
        send_rows(0, v).start()
        if v == 0:
            for copy in small[1:]:
                copy.wait()
            marks = jnp.full((ROWS, LANES), -1, jnp.int32)
            for s in range(capacity):
                marks = jnp.where(lane == s, ids[s], marks)
            post_marks(0, marks, live, sent)

    parent = jnp.full((ROWS, LANES), -1, jnp.int32)
    for s in range(first_rows):
        mine = parents_of[jnp.clip(ids[s], 0, parents_of.shape[0] - 1)]
        parent = jnp.where(lane == s, mine, parent)
    parent = jnp.where(lane < live, parent, -1)

    pool = pool_matrix()
    parents = levels * PAR_DEV
    one_row = lax.broadcasted_iota(jnp.int32, (parents, first_rows), 0)
    one_hot = jnp.where(one_row == parent[0:1, :first_rows], 1.0, 0.0).astype(jnp.bfloat16)
    both_hot = jnp.concatenate([one_hot, one_hot], axis=1)
    plane = EDGE * EDGE
    quarters = cells // (4 * plane)
    slot_of = lax.broadcasted_iota(jnp.int32, (first_rows, plane), 0)
    def restrict_rows(v):
        rows = []
        for q in range(quarters):
            sums = []
            for k in (2 * q, 2 * q + 1):
                a = work[0, v, 0:first_rows, 2 * k * plane:(2 * k + 1) * plane]
                b = work[0, v, 0:first_rows, (2 * k + 1) * plane:(2 * k + 2) * plane]
                sums.append(jnp.where(slot_of < live, a + b, 0.0))
            rows.extend(split(jnp.concatenate(sums, axis=1)))
        pooled = jnp.dot(jnp.concatenate(rows, axis=0), pool, preferred_element_type=jnp.float32)
        for q in range(quarters):
            base = 2 * q * first_rows
            mean = 0.125 * (pooled[base:base + first_rows] + pooled[base + first_rows:base + 2 * first_rows])
            total = jnp.dot(
                both_hot, jnp.concatenate(split(mean), axis=0), preferred_element_type=jnp.float32
            )
            for m in range(levels):
                part[m, v, :, q * LANES:(q + 1) * LANES] = total[PAR_DEV * m:PAR_DEV * (m + 1)]


    def send_a(d):
        to = lax.rem(level + d, levels)
        return pltpu.make_async_remote_copy(
            src_ref=part.at[to], dst_ref=part_in.at[d - 1],
            send_sem=a_send.at[d - 1], recv_sem=a_recv.at[d - 1],
            device_id={"level": to}, device_id_type=MESH,
        )

    def send_b(d):
        to = lax.rem(bal + d, group)
        return pltpu.make_async_remote_copy(
            src_ref=gathered.at[bal], dst_ref=gathered.at[bal],
            send_sem=b_send.at[d - 1], recv_sem=b_recv.at[d - 1],
            device_id={"bal": to}, device_id_type=MESH,
        )

    def parent_sums():
        for v in range(variables):
            restrict_rows(v)

    def send_sums():
        enter_levels()
        for d in range(1, levels):
            send_a(d).start()

    held_count = live
    for r in range(1, rounds):
        kept = held_count - sent
        marks, count = take_marks(r - 1, marks, kept)
        held_count = kept + count
        sent = counts_ref[r]
        post_marks(r, marks, held_count, sent)
        for v in range(variables):
            if r == 1 and v == AHEAD:
                parent_sums()
            if r == 1 and v == SUMS_AT:
                send_sums()
            send_rows(r - 1, v).wait_recv()

            def body(c, carry, v=v, r=r, kept=kept, count=count, held_count=held_count, sent=sent):
                lanes = lanes_of(c)
                arrived = in_rows[r - 1, v, :, lanes[0]]
                merged = []
                for i in range(2):
                    tiles = [load(r - 1, v, t, lanes[i]) for t in range(tile_count(r - 1))]
                    merged.append(merge(tiles, tile_count(r), arrived, kept, count, i == 1))
                    for t in range(tile_count(r)):
                        work[r, v, pl.ds(t * ROWS, ROWS), lanes[i]] = merged[i][t]
                out_rows[r, v, :, lanes[0]] = pack(
                    r, merged[0], merged[1], held_count - sent, held_count
                )
                return carry

            lax.fori_loop(0, chunks, body, 0)
            send_rows(r, v).start()

    for d in range(1, levels):
        send_a(d).wait_recv()
    total = part[level]
    for d in range(1, levels):
        total = total + part_in[d - 1]
    gathered[bal] = total
    for d in range(1, group):
        send_b(d).start()

    kept = held_count - sent
    marks, count = take_marks(rounds - 1, marks, kept)
    new_ids_ref[...] = marks[0:1]
    for v in range(variables):
        send_rows(rounds - 1, v).wait_recv()

        def body(c, carry, v=v):
            lanes = lanes_of(c)
            arrived = in_rows[rounds - 1, v, :, lanes[0]]
            for i in range(2):
                tiles = [load(rounds - 1, v, t, lanes[i]) for t in range(tile_count(rounds - 1))]
                merged = merge(tiles, tile_count(rounds), arrived, kept, count, i == 1)
                for t in range(tile_count(rounds)):
                    size = min(ROWS, capacity - t * ROWS)
                    out_ref[v, pl.ds(t * ROWS, size), lanes[i]] = merged[t][0:size]
            return carry

        lax.fori_loop(0, chunks, body, 0)

    for d in range(1, group):
        send_b(d).wait_recv()
    total = gathered[0]
    for b in range(1, group):
        total = total + gathered[b]
    coarse_ref[...] = total

    for r in range(rounds):
        send_marks(r).wait_send()
        for v in range(variables):
            send_rows(r, v).wait_send()
    for d in range(1, group):
        send_b(d).wait_send()
    for d in range(1, levels):
        send_a(d).wait_send()


def finish(fine_ref, marks_ref, sums_ref, out_ref, ids_ref, coarse_ref, sem):
    variables = fine_ref.shape[0]
    copies = [
        pltpu.make_async_copy(fine_ref.at[v], out_ref.at[v], sem.at[v]) for v in range(variables)
    ]
    copies.append(pltpu.make_async_copy(sums_ref, coarse_ref, sem.at[variables]))
    for copy in copies:
        copy.start()
    ids_ref[...] = marks_ref[0, :ids_ref.shape[0]]
    for copy in copies:
        copy.wait()


def hbm(x):
    return pltpu.with_memory_space_constraint(x, pltpu.HBM)


def per_device(patches, patch_ids, live, counts, parent_of):
    capacity, variables, cells = patches.shape
    group = lax.axis_size("bal")
    levels = lax.axis_size("level")
    rounds = counts.shape[0]
    coarse_cells = cells // 8
    padded = -(-capacity // ROWS) * ROWS
    f32 = jnp.float32
    dma = pltpu.SemaphoreType.DMA
    fine, ids, coarse = pl.pallas_call(
        functools.partial(kernel, group, levels, rounds),
        out_shape=(
            jax.ShapeDtypeStruct((variables, capacity, cells), f32),
            jax.ShapeDtypeStruct((1, LANES), jnp.int32),
            jax.ShapeDtypeStruct((variables, PAR_DEV, coarse_cells), f32),
        ),
        in_specs=[
            pl.BlockSpec(memory_space=pltpu.HBM),
            pl.BlockSpec(memory_space=pltpu.HBM),
            pl.BlockSpec(memory_space=pltpu.SMEM),
            pl.BlockSpec(memory_space=pltpu.HBM),
            pl.BlockSpec(memory_space=pltpu.HBM),
        ],
        out_specs=(
            pl.BlockSpec(memory_space=pltpu.VMEM),
            pl.BlockSpec(memory_space=pltpu.VMEM),
            pl.BlockSpec(memory_space=pltpu.VMEM),
        ),
        scratch_shapes=[
            pltpu.VMEM((rounds, variables, padded, cells), f32),
            pltpu.VMEM((rounds, variables, ROWS, cells // 2), f32),
            pltpu.VMEM((rounds, variables, ROWS, cells // 2), f32),
            pltpu.VMEM((rounds, ROWS, LANES), jnp.int32),
            pltpu.VMEM((rounds, ROWS, LANES), jnp.int32),
            pltpu.VMEM((levels, variables, PAR_DEV, coarse_cells), f32),
            pltpu.VMEM((levels - 1, variables, PAR_DEV, coarse_cells), f32),
            pltpu.VMEM((group, variables, PAR_DEV, coarse_cells), f32),
            pltpu.SMEM((rounds,), jnp.int32),
            pltpu.SMEM(patch_ids.shape, jnp.int32),
            pltpu.SMEM(parent_of.shape, jnp.int32),
            dma((variables,)),
            dma((3,)),
            dma((rounds, variables)),
            dma((rounds, variables)),
            dma((rounds,)),
            dma((rounds,)),
            dma((levels - 1,)),
            dma((levels - 1,)),
            dma((group - 1,)),
            dma((group - 1,)),
            pltpu.SemaphoreType.REGULAR,
            pltpu.SemaphoreType.REGULAR,
        ],
        compiler_params=pltpu.CompilerParams(collective_id=0, has_side_effects=True, vmem_limit_bytes=24 << 20),
    )(hbm(patches.transpose(1, 0, 2)), hbm(patch_ids), live, hbm(counts.reshape(rounds)), hbm(parent_of))
    fine, ids, coarse = pl.pallas_call(
        finish,
        out_shape=(
            jax.ShapeDtypeStruct(fine.shape, f32),
            jax.ShapeDtypeStruct((capacity,), jnp.int32),
            jax.ShapeDtypeStruct(coarse.shape, f32),
        ),
        in_specs=[
            pl.BlockSpec(memory_space=pl.ANY),
            pl.BlockSpec(memory_space=pltpu.VMEM),
            pl.BlockSpec(memory_space=pl.ANY),
        ],
        out_specs=(
            pl.BlockSpec(memory_space=pl.ANY),
            pl.BlockSpec(memory_space=pltpu.VMEM),
            pl.BlockSpec(memory_space=pl.ANY),
        ),
        scratch_shapes=[dma((variables + 1,))],
        compiler_params=pltpu.CompilerParams(vmem_limit_bytes=24 << 20),
    )(fine, ids, coarse)
    return (fine.transpose(1, 0, 2), ids, coarse.transpose(1, 0, 2))


def solution(mesh):
    return jax.shard_map(
        per_device,
        mesh=mesh,
        in_specs=(
            P(("level", "bal"), None, None),
            P(("level", "bal")),
            P(("level", "bal")),
            P(None, ("level", "bal")),
            P(),
        ),
        out_specs=(P(("level", "bal"), None, None), P(("level", "bal")), P("level", None, None)),
        check_vma=False,
    )
```
